1024 devices in a mesh: outer: 64 (over x, z_lo, core), inner: 16 (over y, z_hi).
Axes of the slice: x: 4, y: 8, z: 16 (z_hi: 2, z_lo: 8; z = z_hi * 8 + z_lo), core: 2. Of those that a mesh axis runs over, the one named last changes fastest.
Arguments:
- grads: float32 [64, 16, 524288], P('outer', 'inner'), may hold values from -0.25 to 0.25
- master: float32 [524288], P('inner'), may hold values from -3 to 3
- first_moment: float32 [524288], P('inner'), may hold values from -3 to 3
- second_moment: float32 [524288], P('inner'), may hold values from 0.05 to 1
- ranks: int32 [64], replicated, may hold values from 0 to 63, each once
Outputs:
- new_master: float32 [524288], P('inner')
- new_first: float32 [524288], P('inner')
- new_second: float32 [524288], P('inner')
- weights: bfloat16 [524288], replicated
The draws below stay inside these ranges and needn't reach their ends.
Inputs may be any that keep to these rules, and one draw needn't show every extreme that they name: ranks is a permutation of the replica group indices.
All inputs are finite; a program needn't handle non-finite values.
Results may differ from the reference program's by a relative error of at most 0.006.
Values may be sent and summed in bfloat16 or wider, within the bound.
No kernel may reach another device: no remote copies, remote signals or barrier semaphores. Data moves between devices by JAX's collectives and lax.ppermute only.
A program may use at most 32 MiB of HBM per device.

```python
import math
import jax
import jax.numpy as jnp
from jax import lax

BUCKET = 524288
STEP = 1000
N_OUTER = 64
N_INNER = 16
DEVICES = 1024


def strengthened(values, stream_key, source, target, shards_of, factor):
    owner, partner = [(jnp.arange(values.shape[position]) // (values.shape[position] // shards_of)).reshape([-1 if axis == position else 1 for axis in range(values.ndim)]) for position in (source, target)]
    chosen = jax.random.permutation(stream_key, shards_of)[partner]
    strong = (owner == chosen) | (owner == (partner + shards_of // 2) % shards_of)
    return jnp.where(strong, factor * values, values)


def levels(key, extent, cuts, smallest, high):
    factor_of = 1.0
    for position, shards_of in cuts:
        draws = jax.random.uniform(jax.random.fold_in(jax.random.fold_in(key, 6), position), (shards_of,), jnp.float32, smallest / len(cuts), high / len(cuts))
        factor_of = factor_of * jnp.repeat(jnp.exp(draws), extent[position] // shards_of).reshape((-1,) + (1,) * (len(extent) - 1 - position))
    return factor_of


def gaussian(rng, extent, spread, reach, split=(), dtype=jnp.bfloat16):
    loudness = levels(rng, extent, split, -0.22, 0.18) if split else 1.0
    array = jax.random.normal(rng, extent, jnp.float32) * spread * loudness
    return jnp.minimum(jnp.maximum(array, -reach), reach).astype(dtype)


def gaussian_with(stream_key, shape, spread, bound, cuts, heavy, held_as=jnp.bfloat16):
    drawn = spread * jax.random.normal(stream_key, shape, jnp.float32)
    if cuts:
        drawn = drawn * levels(stream_key, shape, cuts, -0.22, 0.18)
    return jnp.clip(strengthened(drawn, jax.random.fold_in(stream_key, 3), *heavy), -bound, bound).astype(held_as)


def setup_inputs(seed: int = 0) -> dict:
    keys = jax.random.split(jax.random.key(seed), 6)
    return {
        "grads": gaussian_with(keys[0], (N_OUTER, N_INNER, BUCKET), (0.5 * DEVICES ** -0.5), 0.25, ((0, 64), (1, 16)), (0, 2, 64, 4.0), jnp.float32),
        "master": gaussian(keys[1], (BUCKET,), 0.5, 3.0, ((0, 16),), jnp.float32),
        "first_moment": gaussian(keys[2], (BUCKET,), 0.5, 3.0, ((0, 16),), jnp.float32),
        "second_moment": jnp.clip(jnp.exp(math.log(1.0) - 2.9957323 * jax.random.uniform(keys[3], (BUCKET,), jnp.float32) ** levels(keys[3], (BUCKET,), ((0, 16),), -0.2, 0.2)), 0.05, 1.0),
        "ranks": jax.random.permutation(keys[4], N_OUTER).astype(jnp.int32),
    }


def adamw_update(grad, master, first_moment, second_moment):
    new_first = 0.9 * first_moment + 0.1 * grad
    new_second = 0.95 * second_moment + 0.05 * grad * grad
    corr_first = 1.0 - 0.9 ** STEP
    corr_second = 1.0 - 0.95 ** STEP
    direction = new_first / corr_first / (jnp.sqrt(new_second / corr_second) + 1e-05)
    new_master = master - 0.05 * (direction + 0.1 * master)
    return (new_master, new_first, new_second)

def reference(grads, master, first_moment, second_moment, ranks):
    shard_weight = 1.0 + 2.0 * ranks.astype(jnp.float32) / (N_OUTER - 1)

    def accumulate(carry, item):
        block, scale = item
        return (carry + lax.optimization_barrier(jnp.sum(block * scale, axis=0)), None)
    start = jnp.zeros((BUCKET,), jnp.float32)
    grad, _ = lax.scan(accumulate, start, (grads, shard_weight))
    new_master, new_first, new_second = adamw_update(grad, master, first_moment, second_moment)
    return (new_master, new_first, new_second, new_master.astype(jnp.bfloat16))
```

```python
import jax
import jax.numpy as jnp
from jax import lax
from jax.experimental import pallas as pl
from jax.experimental.pallas import tpu as pltpu
from jax.sharding import Mesh, PartitionSpec as P

STEP = 1000
bf16, f32 = jnp.bfloat16, jnp.float32
VMEM = pl.BlockSpec(memory_space=pltpu.VMEM)
SMEM = pl.BlockSpec(memory_space=pltpu.SMEM)
HBM = pl.BlockSpec(memory_space=pltpu.HBM)
SCALE_VMEM = 60 << 20
PARAMS = pltpu.CompilerParams(vmem_limit_bytes=8 << 20)

NX, NY, NC, NZL, NZH = 4, 8, 2, 8, 2
NZ = NZL * NZH
ROWS = 64
SUB = ROWS // NZL
STATE = 4 * SUB


def adamw_update(grad, master, first_moment, second_moment):
    new_first = 0.9 * first_moment + 0.1 * grad
    new_second = 0.95 * second_moment + 0.05 * grad * grad
    corr_first = 1.0 - 0.9**STEP
    corr_second = 1.0 - 0.95**STEP
    direction = new_first / corr_first / (jnp.sqrt(new_second / corr_second) + 1e-05)
    new_master = master - 0.05 * (direction + 0.1 * master)
    return (new_master, new_first, new_second)


def scale_kernel(ranks, grads, master, first, second, own, send, state, buf, sbuf, sem, ssem):
    x, zl, c = lax.axis_index("x"), lax.axis_index("zl"), lax.axis_index("c")
    halves = (1 - c, c)
    copies = [
        [pltpu.make_async_copy(grads.at[y, halves[h]], buf.at[h, y], sem.at[h, y]) for y in range(NY)]
        for h in range(2)
    ]
    at = pl.ds(pl.multiple_of(x * ROWS + zl * SUB, SUB), SUB)
    state_copies = [
        pltpu.make_async_copy(ref.at[at], sbuf.at[i], ssem.at[i])
        for i, ref in enumerate((master, first, second))
    ]
    for h in range(2):
        for copy in copies[h]:
            copy.start()
    for copy in state_copies:
        copy.start()
    outer = (x * NZL + zl) * NC + c
    weight = 1.0 + ranks[outer].astype(f32) * (2.0 / 63.0)
    for h, out in enumerate((send, own)):
        for y in range(NY):
            copies[h][y].wait()
            for k in range(NX):
                out[k, y] = (buf[h, y, pl.ds(k * ROWS, ROWS)] * weight).astype(bf16)
    for copy in state_copies:
        copy.wait()
    high = sbuf[0].astype(bf16)
    low = (sbuf[0] - high.astype(f32)).astype(bf16)
    for i, part in enumerate((high, low, sbuf[1].astype(bf16), sbuf[2].astype(bf16))):
        state[pl.ds(i * SUB, SUB)] = part


def spread_kernel(parts, state, out):
    total = parts[0].astype(f32)
    for y in range(1, NY):
        total += parts[y].astype(f32)
    total = total.astype(bf16)
    for z in range(NZ):
        out[z, pl.ds(0, ROWS)] = total
        out[z, pl.ds(ROWS, STATE)] = state[...]


def update_kernel(parts, weights, grad):
    c = lax.axis_index("c")
    total = parts[0, pl.ds(0, ROWS)].astype(f32)
    for z in range(1, NZ):
        total += parts[z, pl.ds(0, ROWS)].astype(f32)
    grad[...] = total.astype(bf16)
    for j in range(NZL):
        high, low, first, second = (
            parts[NZH * j + c, pl.ds(ROWS + i * SUB, SUB)].astype(f32) for i in range(4)
        )
        piece = adamw_update(total[j * SUB : (j + 1) * SUB], high + low, first, second)[0].astype(bf16)
        for y in range(NY):
            weights[y, pl.ds(j * SUB, SUB)] = piece


def fan_kernel(weights, grad, out):
    for x in range(NX):
        out[x, pl.ds(0, NY)] = weights[...]
        out[x, NY] = grad[...]


def finish_kernel(own, other, master, first, second, weights, new_master, new_first, new_second, sem):
    c, zh = lax.axis_index("c"), lax.axis_index("zh")
    copies = []
    for h, (ref, half) in enumerate(((own, c), (other, 1 - c))):
        for x in range(NX):
            copies.append(
                pltpu.make_async_copy(ref.at[x, pl.ds(0, NY)], weights.at[:, half, x], sem.at[h, x])
            )
    for copy in copies:
        copy.start()
    for x in range(NX):
        at = pl.ds(x * ROWS, ROWS)
        grad = jnp.where(c == zh, own[x, NY].astype(f32), other[x, NY].astype(f32))
        new_master[at], new_first[at], new_second[at] = adamw_update(grad, master[at], first[at], second[at])
    for copy in copies:
        copy.wait()


def shards(grads, master, first_moment, second_moment, ranks):
    shard = (NX * ROWS, 128)
    master, first, second = (a.reshape(shard) for a in (master, first_moment, second_moment))
    half = jax.ShapeDtypeStruct((NX, NY, ROWS, 128), bf16)
    own, send, state = pl.pallas_call(
        scale_kernel,
        out_shape=(half, half, jax.ShapeDtypeStruct((STATE, 128), bf16)),
        in_specs=[SMEM, HBM, HBM, HBM, HBM],
        out_specs=(VMEM, VMEM, VMEM),
        scratch_shapes=[
            pltpu.VMEM((2, NY) + shard, f32),
            pltpu.VMEM((3, SUB, 128), f32),
            pltpu.SemaphoreType.DMA((2, NY)),
            pltpu.SemaphoreType.DMA((3,)),
        ],
        compiler_params=pltpu.CompilerParams(vmem_limit_bytes=SCALE_VMEM),
        name="scale",
    )(ranks, grads.reshape((NY, NC) + shard), master, first, second)
    swap = [(0, 1), (1, 0)]
    got = lax.ppermute(send, "c", swap)
    half_sum = (own.astype(f32) + got.astype(f32)).astype(bf16)
    parts = lax.all_to_all(half_sum, "x", 0, 0, tiled=True)
    parts = jnp.sum(parts.astype(f32), axis=0).astype(bf16)
    parts = lax.all_to_all(parts, "y", 0, 0, tiled=True)
    parts = pl.pallas_call(
        spread_kernel,
        out_shape=jax.ShapeDtypeStruct((NZ, ROWS + STATE, 128), bf16),
        in_specs=[VMEM, VMEM],
        out_specs=VMEM,
        compiler_params=PARAMS,
        name="spread",
    )(parts, state)
    parts = lax.all_to_all(parts, ("zl", "zh"), 0, 0, tiled=True)
    weights, grad = pl.pallas_call(
        update_kernel,
        out_shape=(
            jax.ShapeDtypeStruct((NY, ROWS, 128), bf16),
            jax.ShapeDtypeStruct((ROWS, 128), bf16),
        ),
        in_specs=[VMEM],
        out_specs=(VMEM, VMEM),
        compiler_params=PARAMS,
        name="update",
    )(parts)
    weights = lax.all_to_all(weights, "y", 0, 0, tiled=True)
    fan = pl.pallas_call(
        fan_kernel,
        out_shape=jax.ShapeDtypeStruct((NX, NY + 1, ROWS, 128), bf16),
        in_specs=[VMEM, VMEM],
        out_specs=VMEM,
        compiler_params=PARAMS,
        name="fan",
    )(weights, grad)
    fan = lax.all_to_all(fan, "x", 0, 0, tiled=True)
    other = lax.ppermute(fan, "c", swap)
    out = jax.ShapeDtypeStruct(shard, f32)
    weights, new_master, new_first, new_second = pl.pallas_call(
        finish_kernel,
        out_shape=(jax.ShapeDtypeStruct((NY, NC, NX, ROWS, 128), bf16), out, out, out),
        in_specs=[VMEM] * 5,
        out_specs=(HBM, VMEM, VMEM, VMEM),
        scratch_shapes=[pltpu.SemaphoreType.DMA((2, NX))],
        compiler_params=PARAMS,
        name="finish",
    )(fan, other, master, first, second)
    return (new_master.reshape(-1), new_first.reshape(-1), new_second.reshape(-1), weights.reshape(-1))


def solution(mesh):
    fine = Mesh(mesh.devices.reshape(NX, NZL, NC, NY, NZH), ("x", "zl", "c", "y", "zh"))
    shard = P(("y", "zh"))
    return jax.shard_map(
        shards,
        mesh=fine,
        in_specs=(P(("x", "zl", "c"), ("y", "zh"), None), shard, shard, shard, P()),
        out_specs=(shard, shard, shard, P()),
        check_vma=False,
    )
```

```python
import functools

import jax
import jax.numpy as jnp
from jax import lax
from jax.experimental import pallas as pl
from jax.experimental.pallas import tpu as pltpu
from jax.sharding import Mesh, PartitionSpec as P

STEP = 1000
bf16, f32 = jnp.bfloat16, jnp.float32
VMEM = pl.BlockSpec(memory_space=pltpu.VMEM)
HBM = pl.BlockSpec(memory_space=pltpu.HBM)
SCALE_VMEM = 60 << 20
PARAMS = pltpu.CompilerParams(vmem_limit_bytes=8 << 20)

NX, NY, NC, NZL, NZH = 4, 8, 2, 8, 2
NZ = NZL * NZH
NS = NY * NZH
ROWS = 32


def adamw_update(grad, master, first_moment, second_moment):
    new_first = 0.9 * first_moment + 0.1 * grad
    new_second = 0.95 * second_moment + 0.05 * grad * grad
    corr_first = 1.0 - 0.9**STEP
    corr_second = 1.0 - 0.95**STEP
    direction = new_first / corr_first / (jnp.sqrt(new_second / corr_second) + 1e-05)
    new_master = master - 0.05 * (direction + 0.1 * master)
    return (new_master, new_first, new_second)


def scale_kernel(core, ranks, grads, out, buf, rank, sem, rank_sem):
    x, zl, c = lax.axis_index("x"), lax.axis_index("zl"), lax.axis_index("c")
    half = 1 - c if core else c
    copies = [pltpu.make_async_copy(grads.at[y, :, half], buf.at[y], sem.at[y]) for y in range(NY)]
    rank_copy = pltpu.make_async_copy(ranks, rank, rank_sem)
    rank_copy.start()
    for copy in copies:
        copy.start()
    rank_copy.wait()
    outer = (x * NZL + zl) * NC + c
    weight = 1.0 + rank[outer].astype(f32) * (2.0 / 63.0)
    for y in range(NY):
        copies[y].wait()
        for k in range(NX):
            for z in range(NZH):
                out[k, y, z] = (buf[y, z, pl.ds(k * ROWS, ROWS)] * weight).astype(bf16)


def spread_kernel(parts, out):
    total = parts[0].astype(f32)
    for y in range(1, NY):
        total += parts[y].astype(f32)
    total = total.astype(bf16)
    for z in range(NZL):
        for zh in range(NZH):
            out[z * NZH + zh] = total[zh]


def update_kernel(parts, master, first, second, weights, grad):
    at = pl.ds(pl.multiple_of((lax.axis_index("c") * NX + lax.axis_index("x")) * ROWS, ROWS), ROWS)
    total = parts[0].astype(f32)
    for z in range(1, NZ):
        total += parts[z].astype(f32)
    total = total.astype(bf16)
    grad[...] = total
    piece = adamw_update(total.astype(f32), master[at], first[at], second[at])[0].astype(bf16)
    for s in range(NS):
        weights[s] = piece


def fan_kernel(weights, grad, out):
    for x in range(NX):
        out[x, pl.ds(0, NS)] = weights[...]
        out[x, NS] = grad[...]


def finish_kernel(own, other, master, first, second, weights, new_master, new_first, new_second, sem):
    c = lax.axis_index("c")
    sides = ((own, c), (other, 1 - c))
    copies = [
        pltpu.make_async_copy(ref.at[x, pl.ds(0, NS)], weights.at[:, half, x], sem.at[h, x])
        for h, (ref, half) in enumerate(sides)
        for x in range(NX)
    ]
    for copy in copies:
        copy.start()
    for ref, half in sides:
        for x in range(NX):
            at = pl.ds(pl.multiple_of((half * NX + x) * ROWS, ROWS), ROWS)
            new_master[at], new_first[at], new_second[at] = adamw_update(
                ref[x, NS].astype(f32), master[at], first[at], second[at]
            )
    for copy in copies:
        copy.wait()


def shards(grads, master, first_moment, second_moment, ranks):
    shard = (NC * NX * ROWS, 128)
    master, first, second = (a.reshape(shard) for a in (master, first_moment, second_moment))
    grads = grads.reshape((NY, NZH, NC, NX * ROWS, 128))

    def scaled(core):
        return pl.pallas_call(
            functools.partial(scale_kernel, core),
            out_shape=jax.ShapeDtypeStruct((NX, NY, NZH, ROWS, 128), bf16),
            in_specs=[HBM, HBM],
            out_specs=VMEM,
            scratch_shapes=[
                pltpu.VMEM((NY, NZH, NX * ROWS, 128), f32),
                pltpu.SMEM((64,), jnp.int32),
                pltpu.SemaphoreType.DMA((NY,)),
                pltpu.SemaphoreType.DMA,
            ],
            compiler_params=pltpu.CompilerParams(vmem_limit_bytes=SCALE_VMEM),
            cost_estimate=pl.CostEstimate(flops=1 << 18, bytes_accessed=3 << 19, transcendentals=0),
            name="scale_send" if core else "scale_own",
        )(ranks, grads)

    def local(kernel, out_shape, *operands):
        return pl.pallas_call(
            kernel,
            out_shape=out_shape,
            in_specs=[VMEM] * len(operands),
            out_specs=jax.tree.map(lambda _: VMEM, out_shape),
            compiler_params=PARAMS,
            name=kernel.__name__,
        )(*operands)

    swap = [(0, 1), (1, 0)]
    got = lax.ppermute(scaled(1), "c", swap)
    parts = (scaled(0).astype(f32) + got.astype(f32)).astype(bf16)
    parts = lax.all_to_all(parts, "x", 0, 0, tiled=True)
    parts = jnp.sum(parts.astype(f32), axis=0).astype(bf16)
    parts = lax.all_to_all(parts, "y", 0, 0, tiled=True)
    parts = local(spread_kernel, jax.ShapeDtypeStruct((NZ, ROWS, 128), bf16), parts)
    parts = lax.all_to_all(parts, ("zl", "zh"), 0, 0, tiled=True)
    piece = jax.ShapeDtypeStruct((ROWS, 128), bf16)
    weights, grad = local(
        update_kernel, (jax.ShapeDtypeStruct((NS, ROWS, 128), bf16), piece), parts, master, first, second
    )
    mirrors = [
        [(z % NZL) * NS + y * NZH + z // NZL for y in range(NY) for z in (low, NZ - 1 - low)]
        for low in range(NZL)
    ]
    weights = lax.all_to_all(weights, ("zl", "y", "zh"), 0, 0, tiled=True, axis_index_groups=mirrors)
    fan = local(fan_kernel, jax.ShapeDtypeStruct((NX, NS + 1, ROWS, 128), bf16), weights, grad)
    fan = lax.all_to_all(fan, "x", 0, 0, tiled=True)
    other = lax.ppermute(fan, "c", swap)
    out = jax.ShapeDtypeStruct(shard, f32)
    weights, new_master, new_first, new_second = pl.pallas_call(
        finish_kernel,
        out_shape=(jax.ShapeDtypeStruct((NS, NC, NX, ROWS, 128), bf16), out, out, out),
        in_specs=[VMEM] * 5,
        out_specs=(HBM, VMEM, VMEM, VMEM),
        scratch_shapes=[pltpu.SemaphoreType.DMA((2, NX))],
        compiler_params=PARAMS,
        name="finish",
    )(fan, other, master, first, second)
    return (new_master.reshape(-1), new_first.reshape(-1), new_second.reshape(-1), weights.reshape(-1))


def solution(mesh):
    fine = Mesh(mesh.devices.reshape(NX, NZL, NC, NY, NZH), ("x", "zl", "c", "y", "zh"))
    shard = P(("y", "zh"))
    return jax.shard_map(
        shards,
        mesh=fine,
        in_specs=(P(("x", "zl", "c"), ("y", "zh"), None), shard, shard, shard, P()),
        out_specs=(shard, shard, shard, P()),
        check_vma=False,
    )
```

```python
import functools

import jax
import jax.numpy as jnp
from jax import lax
from jax.experimental import pallas as pl
from jax.experimental.pallas import tpu as pltpu
from jax.sharding import Mesh, PartitionSpec as P

STEP = 1000
bf16, f32 = jnp.bfloat16, jnp.float32
VMEM = pl.BlockSpec(memory_space=pltpu.VMEM)
HBM = pl.BlockSpec(memory_space=pltpu.HBM)
PARAMS = pltpu.CompilerParams(vmem_limit_bytes=8 << 20)

NX, NY, NC, NZL, NZH = 4, 8, 2, 8, 2
NZ = NZL * NZH
NS = NY * NZH
ROWS = 32


def adamw_update(grad, master, first_moment, second_moment):
    new_first = 0.9 * first_moment + 0.1 * grad
    new_second = 0.95 * second_moment + 0.05 * grad * grad
    corr_first = 1.0 - 0.9**STEP
    corr_second = 1.0 - 0.95**STEP
    direction = new_first / corr_first / (jnp.sqrt(new_second / corr_second) + 1e-05)
    new_master = master - 0.05 * (direction + 0.1 * master)
    return (new_master, new_first, new_second)


def scale_kernel(core, ranks, grads, out, buf, rank, sem, rank_sem):
    x, zl, c = lax.axis_index("x"), lax.axis_index("zl"), lax.axis_index("c")
    half = 1 - c if core else c
    copies = [pltpu.make_async_copy(grads.at[y, :, half], buf.at[y], sem.at[y]) for y in range(NY)]
    rank_copy = pltpu.make_async_copy(ranks, rank, rank_sem)
    rank_copy.start()
    for copy in copies:
        copy.start()
    rank_copy.wait()
    outer = (x * NZL + zl) * NC + c
    weight = 1.0 + rank[outer].astype(f32) * (2.0 / 63.0)
    for y in range(NY):
        copies[y].wait()
        for k in range(NX):
            for z in range(NZH):
                out[k, y, z] = (buf[y, z, pl.ds(k * ROWS, ROWS)] * weight).astype(bf16)


def spread_kernel(parts, out):
    total = parts[0].astype(f32)
    for y in range(1, NY):
        total += parts[y].astype(f32)
    total = total.astype(bf16)
    for z in range(NZL):
        for zh in range(NZH):
            out[z * NZH + zh] = total[zh]


def update_kernel(parts, master, first, second, weights, grad):
    at = pl.ds(pl.multiple_of((lax.axis_index("c") * NX + lax.axis_index("x")) * ROWS, ROWS), ROWS)
    total = parts[0].astype(f32)
    for z in range(1, NZ):
        total += parts[z].astype(f32)
    total = total.astype(bf16)
    grad[...] = total
    piece = adamw_update(total.astype(f32), master[at], first[at], second[at])[0].astype(bf16)
    for s in range(NS):
        weights[s] = piece


def combine_kernel(own, got, *out):
    x = lax.axis_index("x")
    for d in range(NX):
        at = lax.rem(x + d, NX)
        out[d][...] = (own[at].astype(f32) + got[at].astype(f32)).astype(bf16)


def join_kernel(weights, grad, out):
    out[pl.ds(0, NS)] = weights[...]
    out[NS] = grad[...]


def stack_kernel(*refs):
    for d in range(NX):
        refs[-1][d] = refs[d][...]


def finish_kernel(own, other, master, first, second, weights, new_master, new_first, new_second, sem):
    x, c = lax.axis_index("x"), lax.axis_index("c")
    sides = ((own, c), (other, 1 - c))
    copies = [
        pltpu.make_async_copy(
            ref.at[d, pl.ds(0, NS)], weights.at[:, half, lax.rem(x + NX - d, NX)], sem.at[h, d]
        )
        for h, (ref, half) in enumerate(sides)
        for d in range(NX)
    ]
    for copy in copies:
        copy.start()
    for ref, half in sides:
        for d in range(NX):
            piece = half * NX + lax.rem(x + NX - d, NX)
            at = pl.ds(pl.multiple_of(piece * ROWS, ROWS), ROWS)
            new_master[at], new_first[at], new_second[at] = adamw_update(
                ref[d, NS].astype(f32), master[at], first[at], second[at]
            )
    for copy in copies:
        copy.wait()


def shards(grads, master, first_moment, second_moment, ranks):
    shard = (NC * NX * ROWS, 128)
    master, first, second = (a.reshape(shard) for a in (master, first_moment, second_moment))
    grads = grads.reshape((NY, NZH, NC, NX * ROWS, 128))

    def scaled(core):
        return pl.pallas_call(
            functools.partial(scale_kernel, core),
            out_shape=jax.ShapeDtypeStruct((NX, NY, NZH, ROWS, 128), bf16),
            in_specs=[HBM, HBM],
            out_specs=VMEM,
            scratch_shapes=[
                pltpu.VMEM((NY, NZH, NX * ROWS, 128), f32),
                pltpu.SMEM((64,), jnp.int32),
                pltpu.SemaphoreType.DMA((NY,)),
                pltpu.SemaphoreType.DMA,
            ],
            compiler_params=pltpu.CompilerParams(vmem_limit_bytes=(60 if core else 52) << 20),
            cost_estimate=pl.CostEstimate(flops=1 << 18, bytes_accessed=3 << 19, transcendentals=0),
            name="scale_send" if core else "scale_own",
        )(ranks, grads)

    def local(kernel, out_shape, *operands):
        return pl.pallas_call(
            kernel,
            out_shape=out_shape,
            in_specs=[VMEM] * len(operands),
            out_specs=jax.tree.map(lambda _: VMEM, out_shape),
            compiler_params=PARAMS,
            name=kernel.__name__,
        )(*operands)

    def along_x(arrays):
        out = {}
        for d in (2, 1, 3):
            out[d] = lax.ppermute(arrays[d - 1], "x", [(i, (i + d) % NX) for i in range(NX)])
        return [out[d] for d in range(1, NX)]

    swap = [(0, 1), (1, 0)]
    got = lax.ppermute(scaled(1), "c", swap)
    quarter = jax.ShapeDtypeStruct((NY, NZH, ROWS, 128), bf16)
    quarters = local(combine_kernel, (quarter,) * NX, scaled(0), got)
    quarters = [quarters[0]] + along_x(quarters[1:])
    parts = sum(q.astype(f32) for q in quarters).astype(bf16)
    parts = lax.all_to_all(parts, "y", 0, 0, tiled=True)
    parts = local(spread_kernel, jax.ShapeDtypeStruct((NZ, ROWS, 128), bf16), parts)
    parts = lax.all_to_all(parts, ("zl", "zh"), 0, 0, tiled=True)
    piece = jax.ShapeDtypeStruct((ROWS, 128), bf16)
    weights, grad = local(
        update_kernel, (jax.ShapeDtypeStruct((NS, ROWS, 128), bf16), piece), parts, master, first, second
    )
    mirrors = [
        [(z % NZL) * NS + y * NZH + z // NZL for y in range(NY) for z in (low, NZ - 1 - low)]
        for low in range(NZL)
    ]
    weights = lax.all_to_all(weights, ("zl", "y", "zh"), 0, 0, tiled=True, axis_index_groups=mirrors)
    fan = local(join_kernel, jax.ShapeDtypeStruct((NS + 1, ROWS, 128), bf16), weights, grad)
    fan = local(
        stack_kernel, jax.ShapeDtypeStruct((NX, NS + 1, ROWS, 128), bf16), fan, *along_x([fan] * (NX - 1))
    )
    other = lax.ppermute(fan, "c", swap)
    out = jax.ShapeDtypeStruct(shard, f32)
    weights, new_master, new_first, new_second = pl.pallas_call(
        finish_kernel,
        out_shape=(jax.ShapeDtypeStruct((NS, NC, NX, ROWS, 128), bf16), out, out, out),
        in_specs=[VMEM] * 5,
        out_specs=(HBM, VMEM, VMEM, VMEM),
        scratch_shapes=[pltpu.SemaphoreType.DMA((2, NX))],
        compiler_params=PARAMS,
        name="finish",
    )(fan, other, master, first, second)
    return (new_master.reshape(-1), new_first.reshape(-1), new_second.reshape(-1), weights.reshape(-1))


def solution(mesh):
    fine = Mesh(mesh.devices.reshape(NX, NZL, NC, NY, NZH), ("x", "zl", "c", "y", "zh"))
    shard = P(("y", "zh"))
    return jax.shard_map(
        shards,
        mesh=fine,
        in_specs=(P(("x", "zl", "c"), ("y", "zh"), None), shard, shard, shard, P()),
        out_specs=(shard, shard, shard, P()),
        check_vma=False,
    )
```

```python
import functools

import jax
import jax.numpy as jnp
from jax import lax
from jax.experimental import pallas as pl
from jax.experimental.pallas import tpu as pltpu
from jax.sharding import Mesh, PartitionSpec as P

STEP = 1000
bf16, f32 = jnp.bfloat16, jnp.float32
VMEM = pl.BlockSpec(memory_space=pltpu.VMEM)
HBM = pl.BlockSpec(memory_space=pltpu.HBM)
PARAMS = pltpu.CompilerParams(vmem_limit_bytes=8 << 20)

NX, NY, NC, NZL, NZH = 4, 8, 2, 8, 2
NZ = NZL * NZH
NS = NY * NZH
ROWS = 32


def adamw_update(grad, master, first_moment, second_moment):
    new_first = 0.9 * first_moment + 0.1 * grad
    new_second = 0.95 * second_moment + 0.05 * grad * grad
    corr_first = 1.0 - 0.9**STEP
    corr_second = 1.0 - 0.95**STEP
    direction = new_first / corr_first / (jnp.sqrt(new_second / corr_second) + 1e-05)
    new_master = master - 0.05 * (direction + 0.1 * master)
    return (new_master, new_first, new_second)


def scale_kernel(core, ranks, grads, out, buf, rank, sem, rank_sem):
    x, zl, c = lax.axis_index("x"), lax.axis_index("zl"), lax.axis_index("c")
    half = 1 - c if core else c
    copies = [pltpu.make_async_copy(grads.at[y, :, half], buf.at[y], sem.at[y]) for y in range(NY)]
    rank_copy = pltpu.make_async_copy(ranks, rank, rank_sem)
    rank_copy.start()
    for copy in copies:
        copy.start()
    rank_copy.wait()
    outer = (x * NZL + zl) * NC + c
    weight = 1.0 + rank[outer].astype(f32) * (2.0 / 63.0)
    for y in range(NY):
        copies[y].wait()
        for k in range(NX):
            for z in range(NZH):
                out[k, y, z] = (buf[y, z, pl.ds(k * ROWS, ROWS)] * weight).astype(bf16)


def combine_kernel(own, got, out):
    for x in range(NX):
        out[x] = (own[x].astype(f32) + got[x].astype(f32)).astype(bf16)


def spread_kernel(parts, out):
    total = parts[0].astype(f32)
    for y in range(1, NY):
        total += parts[y].astype(f32)
    total = total.astype(bf16)
    for z in range(NZL):
        for zh in range(NZH):
            out[z * NZH + zh] = total[zh]


def update_kernel(parts, master, first, second, weights, grad):
    at = pl.ds(pl.multiple_of((lax.axis_index("c") * NX + lax.axis_index("x")) * ROWS, ROWS), ROWS)
    total = parts[0].astype(f32)
    for z in range(1, NZ):
        total += parts[z].astype(f32)
    total = total.astype(bf16)
    grad[...] = total
    piece = adamw_update(total.astype(f32), master[at], first[at], second[at])[0].astype(bf16)
    for s in range(NS):
        weights[s] = piece


def fan_kernel(weights, grad, out):
    for x in range(NX):
        out[x, pl.ds(0, NS)] = weights[...]
        out[x, NS] = grad[...]


def finish_kernel(partner, *refs):
    ref, master, first, second, *_, weights, new_master, new_first, new_second, state, sem, state_sem = refs
    half = lax.axis_index("c")
    half = 1 - half if partner else half
    copies = [
        pltpu.make_async_copy(ref.at[x, pl.ds(0, NS)], weights.at[:, half, x], sem.at[x]) for x in range(NX)
    ]
    for copy in copies:
        copy.start()
    rows = pl.ds(pl.multiple_of(half * NX * ROWS, ROWS), NX * ROWS)
    for x in range(NX):
        at = pl.ds(pl.multiple_of((half * NX + x) * ROWS, ROWS), ROWS)
        new = adamw_update(ref[x, NS].astype(f32), master[at], first[at], second[at])
        for i in range(3):
            state[i, pl.ds(x * ROWS, ROWS)] = new[i]
    for i, out in enumerate((new_master, new_first, new_second)):
        copies.append(pltpu.make_async_copy(state.at[i], out.at[rows], state_sem.at[i]))
        copies[-1].start()
    for copy in copies:
        copy.wait()


def shards(grads, master, first_moment, second_moment, ranks):
    shard = (NC * NX * ROWS, 128)
    master, first, second = (a.reshape(shard) for a in (master, first_moment, second_moment))
    grads = grads.reshape((NY, NZH, NC, NX * ROWS, 128))

    def scaled(core):
        return pl.pallas_call(
            functools.partial(scale_kernel, core),
            out_shape=jax.ShapeDtypeStruct((NX, NY, NZH, ROWS, 128), bf16),
            in_specs=[HBM, HBM],
            out_specs=VMEM,
            scratch_shapes=[
                pltpu.VMEM((NY, NZH, NX * ROWS, 128), f32),
                pltpu.SMEM((64,), jnp.int32),
                pltpu.SemaphoreType.DMA((NY,)),
                pltpu.SemaphoreType.DMA,
            ],
            compiler_params=pltpu.CompilerParams(vmem_limit_bytes=(60 if core else 52) << 20),
            cost_estimate=pl.CostEstimate(flops=1 << 18, bytes_accessed=3 << 19, transcendentals=0),
            name="scale_send" if core else "scale_own",
        )(ranks, grads)

    def local(kernel, out_shape, *operands):
        return pl.pallas_call(
            kernel,
            out_shape=out_shape,
            in_specs=[VMEM] * len(operands),
            out_specs=jax.tree.map(lambda _: VMEM, out_shape),
            compiler_params=PARAMS,
            name=kernel.__name__,
        )(*operands)

    swap = [(0, 1), (1, 0)]
    got = lax.ppermute(scaled(1), "c", swap)
    half = jax.ShapeDtypeStruct((NX, NY, NZH, ROWS, 128), bf16)
    parts = local(combine_kernel, half, scaled(0), got)
    parts = lax.all_to_all(parts, "x", 0, 0, tiled=True)
    parts = jnp.sum(parts.astype(f32), axis=0).astype(bf16)
    parts = lax.all_to_all(parts, "y", 0, 0, tiled=True)
    parts = local(spread_kernel, jax.ShapeDtypeStruct((NZ, ROWS, 128), bf16), parts)
    parts = lax.all_to_all(parts, ("zl", "zh"), 0, 0, tiled=True)
    piece = jax.ShapeDtypeStruct((ROWS, 128), bf16)
    weights, grad = local(
        update_kernel, (jax.ShapeDtypeStruct((NS, ROWS, 128), bf16), piece), parts, master, first, second
    )
    mirrors = [
        [(z % NZL) * NS + y * NZH + z // NZL for y in range(NY) for z in (low, NZ - 1 - low)]
        for low in range(NZL)
    ]
    weights = lax.all_to_all(weights, ("zl", "y", "zh"), 0, 0, tiled=True, axis_index_groups=mirrors)
    fan = local(fan_kernel, jax.ShapeDtypeStruct((NX, NS + 1, ROWS, 128), bf16), weights, grad)
    fan = lax.all_to_all(fan, "x", 0, 0, tiled=True)
    other = lax.ppermute(fan, "c", swap)
    out = jax.ShapeDtypeStruct(shard, f32)
    outs = ()
    for partner, ref in enumerate((fan, other)):
        outs = pl.pallas_call(
            functools.partial(finish_kernel, partner),
            out_shape=(jax.ShapeDtypeStruct((NS, NC, NX, ROWS, 128), bf16), out, out, out),
            in_specs=[VMEM] * 4 + [HBM] * len(outs),
            out_specs=(HBM,) * 4,
            input_output_aliases={4 + i: i for i in range(len(outs))},
            scratch_shapes=[
                pltpu.VMEM((3, NX * ROWS, 128), f32),
                pltpu.SemaphoreType.DMA((NX,)),
                pltpu.SemaphoreType.DMA((3,)),
            ],
            compiler_params=PARAMS,
            cost_estimate=pl.CostEstimate(flops=1 << 18, bytes_accessed=3 << 19, transcendentals=0),
            name="finish_partner" if partner else "finish_own",
        )(ref, master, first, second, *outs)
    weights, new_master, new_first, new_second = outs
    return (new_master.reshape(-1), new_first.reshape(-1), new_second.reshape(-1), weights.reshape(-1))


def solution(mesh):
    fine = Mesh(mesh.devices.reshape(NX, NZL, NC, NY, NZH), ("x", "zl", "c", "y", "zh"))
    shard = P(("y", "zh"))
    return jax.shard_map(
        shards,
        mesh=fine,
        in_specs=(P(("x", "zl", "c"), ("y", "zh"), None), shard, shard, shard, P()),
        out_specs=(shard, shard, shard, P()),
        check_vma=False,
    )
```

```python
import functools

import jax
import jax.numpy as jnp
from jax import lax
from jax.experimental import pallas as pl
from jax.experimental.pallas import tpu as pltpu
from jax.sharding import Mesh, PartitionSpec as P

STEP = 1000
bf16, f32 = jnp.bfloat16, jnp.float32
VMEM = pl.BlockSpec(memory_space=pltpu.VMEM)
HBM = pl.BlockSpec(memory_space=pltpu.HBM)
PARAMS = pltpu.CompilerParams(vmem_limit_bytes=8 << 20)

NX, NY, NC, NZL, NZH = 4, 8, 2, 8, 2
NZ = NZL * NZH
NS = NY * NZH
ROWS = 32


def adamw_update(grad, master, first_moment, second_moment):
    new_first = 0.9 * first_moment + 0.1 * grad
    new_second = 0.95 * second_moment + 0.05 * grad * grad
    corr_first = 1.0 - 0.9**STEP
    corr_second = 1.0 - 0.95**STEP
    direction = new_first / corr_first / (jnp.sqrt(new_second / corr_second) + 1e-05)
    new_master = master - 0.05 * (direction + 0.1 * master)
    return (new_master, new_first, new_second)


def scale_kernel(core, ranks, grads, out, buf, rank, sem, rank_sem):
    x, zl, c = lax.axis_index("x"), lax.axis_index("zl"), lax.axis_index("c")
    half = 1 - c if core else c
    copies = [pltpu.make_async_copy(grads.at[y, :, half], buf.at[y], sem.at[y]) for y in range(NY)]
    rank_copy = pltpu.make_async_copy(ranks, rank, rank_sem)
    rank_copy.start()
    for copy in copies:
        copy.start()
    rank_copy.wait()
    outer = (x * NZL + zl) * NC + c
    weight = 1.0 + rank[outer].astype(f32) * (2.0 / 63.0)
    for y in range(NY):
        copies[y].wait()
        for k in range(NX):
            for z in range(NZH):
                out[k, y, z] = (buf[y, z, pl.ds(k * ROWS, ROWS)] * weight).astype(bf16)


def combine_kernel(own, got, out):
    for x in range(NX):
        out[x] = (own[x].astype(f32) + got[x].astype(f32)).astype(bf16)


def spread_kernel(parts, out):
    total = parts[0].astype(f32)
    for y in range(1, NY):
        total += parts[y].astype(f32)
    total = total.astype(bf16)
    for z in range(NZL):
        for zh in range(NZH):
            out[z * NZH + zh] = total[zh]


def update_kernel(parts, master, first, second, weights, grad):
    at = pl.ds(pl.multiple_of((lax.axis_index("c") * NX + lax.axis_index("x")) * ROWS, ROWS), ROWS)
    total = parts[0].astype(f32)
    for z in range(1, NZ):
        total += parts[z].astype(f32)
    total = total.astype(bf16)
    grad[...] = total
    piece = adamw_update(total.astype(f32), master[at], first[at], second[at])[0].astype(bf16)
    for s in range(NS):
        weights[s] = piece


def fan_kernel(weights, grad, out):
    for x in range(NX):
        out[x, pl.ds(0, NS)] = weights[...]
        out[x, NS] = grad[...]


def finish_kernel(partner, *refs):
    ref, master, first, second, *_, weights, new_master, new_first, new_second, state, sem, state_sem = refs
    half = lax.axis_index("c")
    half = 1 - half if partner else half
    copies = [
        pltpu.make_async_copy(ref.at[x, pl.ds(0, NS)], weights.at[:, half, x], sem.at[x]) for x in range(NX)
    ]
    for copy in copies:
        copy.start()
    rows = pl.ds(pl.multiple_of(half * NX * ROWS, ROWS), NX * ROWS)
    for x in range(NX):
        at = pl.ds(pl.multiple_of((half * NX + x) * ROWS, ROWS), ROWS)
        new = adamw_update(ref[x, NS].astype(f32), master[at], first[at], second[at])
        for i in range(3):
            state[i, pl.ds(x * ROWS, ROWS)] = new[i]
    for i, out in enumerate((new_master, new_first, new_second)):
        copies.append(pltpu.make_async_copy(state.at[i], out.at[rows], state_sem.at[i]))
        copies[-1].start()
    for copy in copies:
        copy.wait()


def shards(grads, master, first_moment, second_moment, ranks):
    shard = (NC * NX * ROWS, 128)
    master, first, second = (a.reshape(shard) for a in (master, first_moment, second_moment))
    grads = grads.reshape((NY, NZH, NC, NX * ROWS, 128))

    def scaled(core):
        return pl.pallas_call(
            functools.partial(scale_kernel, core),
            out_shape=jax.ShapeDtypeStruct((NX, NY, NZH, ROWS, 128), bf16),
            in_specs=[HBM, HBM],
            out_specs=VMEM,
            scratch_shapes=[
                pltpu.VMEM((NY, NZH, NX * ROWS, 128), f32),
                pltpu.SMEM((64,), jnp.int32),
                pltpu.SemaphoreType.DMA((NY,)),
                pltpu.SemaphoreType.DMA,
            ],
            compiler_params=pltpu.CompilerParams(vmem_limit_bytes=(60 if core else 52) << 20),
            cost_estimate=pl.CostEstimate(flops=1 << 18, bytes_accessed=3 << 19, transcendentals=0),
            name="scale_send" if core else "scale_own",
        )(ranks, grads)

    def local(kernel, out_shape, *operands):
        return pl.pallas_call(
            kernel,
            out_shape=out_shape,
            in_specs=[VMEM] * len(operands),
            out_specs=jax.tree.map(lambda _: VMEM, out_shape),
            compiler_params=PARAMS,
            name=kernel.__name__,
        )(*operands)

    swap = [(0, 1), (1, 0)]
    got = lax.ppermute(scaled(1), "c", swap)
    half = jax.ShapeDtypeStruct((NX, NY, NZH, ROWS, 128), bf16)
    parts = local(combine_kernel, half, scaled(0), got)
    parts = lax.all_to_all(parts, "x", 0, 0, tiled=True)
    parts = jnp.sum(parts.astype(f32), axis=0).astype(bf16)
    parts = lax.all_to_all(parts, "y", 0, 0, tiled=True)
    parts = local(spread_kernel, jax.ShapeDtypeStruct((NZ, ROWS, 128), bf16), parts)
    parts = lax.all_to_all(parts, ("zl", "zh"), 0, 0, tiled=True)
    piece = jax.ShapeDtypeStruct((ROWS, 128), bf16)
    weights, grad = local(
        update_kernel, (jax.ShapeDtypeStruct((NS, ROWS, 128), bf16), piece), parts, master, first, second
    )
    pairs = [
        [(z % NZL) * NS + y * NZH + z // NZL for y in range(NY) for z in (low, (low + far) % NZ)]
        for low in range(NZL)
        for far in (NZL // 2 if low >= NZL // 2 else NZ - NZL // 2,)
    ]
    weights = lax.all_to_all(weights, ("zl", "y", "zh"), 0, 0, tiled=True, axis_index_groups=pairs)
    fan = local(fan_kernel, jax.ShapeDtypeStruct((NX, NS + 1, ROWS, 128), bf16), weights, grad)
    fan = lax.all_to_all(fan, "x", 0, 0, tiled=True)
    other = lax.ppermute(fan, "c", swap)
    out = jax.ShapeDtypeStruct(shard, f32)
    outs = ()
    for partner, ref in enumerate((fan, other)):
        outs = pl.pallas_call(
            functools.partial(finish_kernel, partner),
            out_shape=(jax.ShapeDtypeStruct((NS, NC, NX, ROWS, 128), bf16), out, out, out),
            in_specs=[VMEM] * 4 + [HBM] * len(outs),
            out_specs=(HBM,) * 4,
            input_output_aliases={4 + i: i for i in range(len(outs))},
            scratch_shapes=[
                pltpu.VMEM((3, NX * ROWS, 128), f32),
                pltpu.SemaphoreType.DMA((NX,)),
                pltpu.SemaphoreType.DMA((3,)),
            ],
            compiler_params=PARAMS,
            cost_estimate=pl.CostEstimate(flops=1 << 18, bytes_accessed=3 << 19, transcendentals=0),
            name="finish_partner" if partner else "finish_own",
        )(ref, master, first, second, *outs)
    weights, new_master, new_first, new_second = outs
    return (new_master.reshape(-1), new_first.reshape(-1), new_second.reshape(-1), weights.reshape(-1))


def solution(mesh):
    fine = Mesh(mesh.devices.reshape(NX, NZL, NC, NY, NZH), ("x", "zl", "c", "y", "zh"))
    shard = P(("y", "zh"))
    return jax.shard_map(
        shards,
        mesh=fine,
        in_specs=(P(("x", "zl", "c"), ("y", "zh"), None), shard, shard, shard, P()),
        out_specs=(shard, shard, shard, P()),
        check_vma=False,
    )
```

```python
import functools

import jax
import jax.numpy as jnp
from jax import lax
from jax.experimental import pallas as pl
from jax.experimental.pallas import tpu as pltpu
from jax.sharding import Mesh, PartitionSpec as P

STEP = 1000
bf16, f32 = jnp.bfloat16, jnp.float32
VMEM = pl.BlockSpec(memory_space=pltpu.VMEM)
HBM = pl.BlockSpec(memory_space=pltpu.HBM)
PARAMS = pltpu.CompilerParams(vmem_limit_bytes=8 << 20)

NX, NY, NC, NZL, NZH = 4, 8, 2, 8, 2
NZ = NZL * NZH
NS = NY * NZH
ROWS = 32


def adamw_update(grad, master, first_moment, second_moment):
    new_first = 0.9 * first_moment + 0.1 * grad
    new_second = 0.95 * second_moment + 0.05 * grad * grad
    corr_first = 1.0 - 0.9**STEP
    corr_second = 1.0 - 0.95**STEP
    direction = new_first / corr_first / (jnp.sqrt(new_second / corr_second) + 1e-05)
    new_master = master - 0.05 * (direction + 0.1 * master)
    return (new_master, new_first, new_second)


def scale_kernel(core, ranks, grads, out, buf, rank, sem, rank_sem, *send):
    x, zl, c = lax.axis_index("x"), lax.axis_index("zl"), lax.axis_index("c")
    half = 1 - c if core else c
    copies = [pltpu.make_async_copy(grads.at[y, :, half], buf.at[y], sem.at[y]) for y in range(NY)]
    rank_copy = pltpu.make_async_copy(ranks, rank, rank_sem)
    rank_copy.start()
    for copy in copies:
        copy.start()
    rank_copy.wait()
    outer = (x * NZL + zl) * NC + c
    weight = 1.0 + rank[outer].astype(f32) * (2.0 / 63.0)
    stage = send[0] if core else out
    sends = []
    for y in range(NY):
        copies[y].wait()
        for k in range(NX):
            for z in range(NZH):
                stage[k, y, z] = (buf[y, z, pl.ds(k * ROWS, ROWS)] * weight).astype(bf16)
        if core:
            sends.append(pltpu.make_async_copy(stage.at[:, y], out.at[:, y], send[1].at[y]))
            sends[-1].start()
    for copy in sends:
        copy.wait()


def combine_kernel(own, got, out):
    for x in range(NX):
        out[x] = (own[x].astype(f32) + got[x].astype(f32)).astype(bf16)


def spread_kernel(parts, out):
    total = parts[0].astype(f32)
    for xy in range(1, NX * NY):
        total += parts[xy].astype(f32)
    total = total.astype(bf16)
    for z in range(NZL):
        for zh in range(NZH):
            out[z * NZH + zh] = total[zh]


def update_kernel(parts, master, first, second, weights, grad):
    at = pl.ds(pl.multiple_of((lax.axis_index("c") * NX + lax.axis_index("x")) * ROWS, ROWS), ROWS)
    total = parts[0].astype(f32)
    for z in range(1, NZ):
        total += parts[z].astype(f32)
    total = total.astype(bf16)
    grad[...] = total
    piece = adamw_update(total.astype(f32), master[at], first[at], second[at])[0].astype(bf16)
    for s in range(NS):
        weights[s] = piece


def fan_kernel(weights, grad, out):
    for x in range(NX):
        out[x, pl.ds(0, NS)] = weights[...]
        out[x, NS] = grad[...]


def finish_kernel(partner, *refs):
    ref, master, first, second, *_, weights, new_master, new_first, new_second, state, sem, state_sem = refs
    half = lax.axis_index("c")
    half = 1 - half if partner else half
    copies = [
        pltpu.make_async_copy(ref.at[x, pl.ds(0, NS)], weights.at[:, half, x], sem.at[x]) for x in range(NX)
    ]
    for copy in copies:
        copy.start()
    rows = pl.ds(pl.multiple_of(half * NX * ROWS, ROWS), NX * ROWS)
    for x in range(NX):
        at = pl.ds(pl.multiple_of((half * NX + x) * ROWS, ROWS), ROWS)
        new = adamw_update(ref[x, NS].astype(f32), master[at], first[at], second[at])
        for i in range(3):
            state[i, pl.ds(x * ROWS, ROWS)] = new[i]
    for i, out in enumerate((new_master, new_first, new_second)):
        copies.append(pltpu.make_async_copy(state.at[i], out.at[rows], state_sem.at[i]))
        copies[-1].start()
    for copy in copies:
        copy.wait()


def shards(grads, master, first_moment, second_moment, ranks):
    shard = (NC * NX * ROWS, 128)
    master, first, second = (a.reshape(shard) for a in (master, first_moment, second_moment))
    grads = grads.reshape((NY, NZH, NC, NX * ROWS, 128))

    half = (NX, NY, NZH, ROWS, 128)

    def scaled(core):
        return pl.pallas_call(
            functools.partial(scale_kernel, core),
            out_shape=jax.ShapeDtypeStruct(half, bf16),
            in_specs=[HBM, HBM],
            out_specs=HBM if core else VMEM,
            scratch_shapes=[
                pltpu.VMEM((NY, NZH, NX * ROWS, 128), f32),
                pltpu.SMEM((64,), jnp.int32),
                pltpu.SemaphoreType.DMA((NY,)),
                pltpu.SemaphoreType.DMA,
            ]
            + [pltpu.VMEM(half, bf16), pltpu.SemaphoreType.DMA((NY,))] * core,
            compiler_params=pltpu.CompilerParams(vmem_limit_bytes=(60 if core else 52) << 20),
            cost_estimate=pl.CostEstimate(flops=1 << 18, bytes_accessed=3 << 19, transcendentals=0),
            name="scale_send" if core else "scale_own",
        )(ranks, grads)

    def local(kernel, out_shape, *operands):
        return pl.pallas_call(
            kernel,
            out_shape=out_shape,
            in_specs=[VMEM] * len(operands),
            out_specs=jax.tree.map(lambda _: VMEM, out_shape),
            compiler_params=PARAMS,
            name=kernel.__name__,
        )(*operands)

    swap = [(0, 1), (1, 0)]
    got = lax.ppermute(scaled(1), "c", swap)
    parts = local(combine_kernel, jax.ShapeDtypeStruct(half, bf16), scaled(0), got)
    parts = parts.reshape((NX * NY, NZH, ROWS, 128))
    parts = lax.all_to_all(parts, ("x", "y"), 0, 0, tiled=True)
    parts = local(spread_kernel, jax.ShapeDtypeStruct((NZ, ROWS, 128), bf16), parts)
    parts = lax.all_to_all(parts, ("zl", "zh"), 0, 0, tiled=True)
    piece = jax.ShapeDtypeStruct((ROWS, 128), bf16)
    weights, grad = local(
        update_kernel, (jax.ShapeDtypeStruct((NS, ROWS, 128), bf16), piece), parts, master, first, second
    )
    mirrors = [
        [(z % NZL) * NS + y * NZH + z // NZL for y in range(NY) for z in (low, NZ - 1 - low)]
        for low in range(NZL)
    ]
    weights = lax.all_to_all(weights, ("zl", "y", "zh"), 0, 0, tiled=True, axis_index_groups=mirrors)
    fan = local(fan_kernel, jax.ShapeDtypeStruct((NX, NS + 1, ROWS, 128), bf16), weights, grad)
    fan = lax.all_to_all(fan, "x", 0, 0, tiled=True)
    other = lax.ppermute(fan, "c", swap)
    out = jax.ShapeDtypeStruct(shard, f32)
    outs = ()
    for partner, ref in enumerate((fan, other)):
        outs = pl.pallas_call(
            functools.partial(finish_kernel, partner),
            out_shape=(jax.ShapeDtypeStruct((NS, NC, NX, ROWS, 128), bf16), out, out, out),
            in_specs=[VMEM] * 4 + [HBM] * len(outs),
            out_specs=(HBM,) * 4,
            input_output_aliases={4 + i: i for i in range(len(outs))},
            scratch_shapes=[
                pltpu.VMEM((3, NX * ROWS, 128), f32),
                pltpu.SemaphoreType.DMA((NX,)),
                pltpu.SemaphoreType.DMA((3,)),
            ],
            compiler_params=PARAMS,
            cost_estimate=pl.CostEstimate(flops=1 << 18, bytes_accessed=3 << 19, transcendentals=0),
            name="finish_partner" if partner else "finish_own",
        )(ref, master, first, second, *outs)
    weights, new_master, new_first, new_second = outs
    return (new_master.reshape(-1), new_first.reshape(-1), new_second.reshape(-1), weights.reshape(-1))


def solution(mesh):
    fine = Mesh(mesh.devices.reshape(NX, NZL, NC, NY, NZH), ("x", "zl", "c", "y", "zh"))
    shard = P(("y", "zh"))
    return jax.shard_map(
        shards,
        mesh=fine,
        in_specs=(P(("x", "zl", "c"), ("y", "zh"), None), shard, shard, shard, P()),
        out_specs=(shard, shard, shard, P()),
        check_vma=False,
    )
```

```python
import functools

import jax
import jax.numpy as jnp
from jax import lax
from jax.experimental import pallas as pl
from jax.experimental.pallas import tpu as pltpu
from jax.sharding import Mesh, PartitionSpec as P

STEP = 1000
bf16, f32 = jnp.bfloat16, jnp.float32
VMEM = pl.BlockSpec(memory_space=pltpu.VMEM)
HBM = pl.BlockSpec(memory_space=pltpu.HBM)
PARAMS = pltpu.CompilerParams(vmem_limit_bytes=8 << 20)

NX, NY, NC, NZL, NZH = 4, 8, 2, 8, 2
NZ = NZL * NZH
NS = NY * NZH
ROWS = 32


def adamw_update(grad, master, first_moment, second_moment):
    new_first = 0.9 * first_moment + 0.1 * grad
    new_second = 0.95 * second_moment + 0.05 * grad * grad
    corr_first = 1.0 - 0.9**STEP
    corr_second = 1.0 - 0.95**STEP
    direction = new_first / corr_first / (jnp.sqrt(new_second / corr_second) + 1e-05)
    new_master = master - 0.05 * (direction + 0.1 * master)
    return (new_master, new_first, new_second)


def scale_kernel(core, ranks, grads, out, buf, rank, sem, rank_sem, *send):
    x, zl, c = lax.axis_index("x"), lax.axis_index("zl"), lax.axis_index("c")
    half = 1 - c if core else c
    copies = [pltpu.make_async_copy(grads.at[y, :, half], buf.at[y], sem.at[y]) for y in range(NY)]
    rank_copy = pltpu.make_async_copy(ranks, rank, rank_sem)
    rank_copy.start()
    for copy in copies:
        copy.start()
    rank_copy.wait()
    outer = (x * NZL + zl) * NC + c
    weight = 1.0 + rank[outer].astype(f32) * (2.0 / 63.0)
    stage = send[0] if core else out
    sends = []
    for y in range(NY):
        copies[y].wait()
        for k in range(NX):
            for z in range(NZH):
                stage[k, y, z] = (buf[y, z, pl.ds(k * ROWS, ROWS)] * weight).astype(bf16)
        if core:
            sends.append(pltpu.make_async_copy(stage.at[:, y], out.at[:, y], send[1].at[y]))
            sends[-1].start()
    for copy in sends:
        copy.wait()


def combine_kernel(own, got, out):
    for x in range(NX):
        out[x] = (own[x].astype(f32) + got[x].astype(f32)).astype(bf16)


def spread_kernel(parts, out):
    total = parts[0].astype(f32)
    for y in range(1, NY):
        total += parts[y].astype(f32)
    total = total.astype(bf16)
    for z in range(NZL):
        for zh in range(NZH):
            out[z * NZH + zh] = total[zh]


def update_kernel(parts, master, first, second, weights, grad):
    at = pl.ds(pl.multiple_of((lax.axis_index("c") * NX + lax.axis_index("x")) * ROWS, ROWS), ROWS)
    total = parts[0].astype(f32)
    for z in range(1, NZ):
        total += parts[z].astype(f32)
    total = total.astype(bf16)
    grad[...] = total
    piece = adamw_update(total.astype(f32), master[at], first[at], second[at])[0].astype(bf16)
    for s in range(NS):
        weights[s] = piece


def fan_kernel(weights, grad, out):
    for x in range(NX):
        out[x, pl.ds(0, NS)] = weights[...]
        out[x, NS] = grad[...]


def finish_kernel(partner, *refs):
    ref, master, first, second, *_, weights, new_master, new_first, new_second, state, sem, state_sem = refs
    half = lax.axis_index("c")
    half = 1 - half if partner else half
    copies = [
        pltpu.make_async_copy(ref.at[x, pl.ds(0, NS)], weights.at[:, half, x], sem.at[x]) for x in range(NX)
    ]
    for copy in copies:
        copy.start()
    rows = pl.ds(pl.multiple_of(half * NX * ROWS, ROWS), NX * ROWS)
    for x in range(NX):
        at = pl.ds(pl.multiple_of((half * NX + x) * ROWS, ROWS), ROWS)
        new = adamw_update(ref[x, NS].astype(f32), master[at], first[at], second[at])
        for i in range(3):
            state[i, pl.ds(x * ROWS, ROWS)] = new[i]
    for i, out in enumerate((new_master, new_first, new_second)):
        copies.append(pltpu.make_async_copy(state.at[i], out.at[rows], state_sem.at[i]))
        copies[-1].start()
    for copy in copies:
        copy.wait()


def shards(grads, master, first_moment, second_moment, ranks):
    shard = (NC * NX * ROWS, 128)
    master, first, second = (a.reshape(shard) for a in (master, first_moment, second_moment))
    grads = grads.reshape((NY, NZH, NC, NX * ROWS, 128))

    half = (NX, NY, NZH, ROWS, 128)

    def scaled(core):
        return pl.pallas_call(
            functools.partial(scale_kernel, core),
            out_shape=jax.ShapeDtypeStruct(half, bf16),
            in_specs=[HBM, HBM],
            out_specs=HBM if core else VMEM,
            scratch_shapes=[
                pltpu.VMEM((NY, NZH, NX * ROWS, 128), f32),
                pltpu.SMEM((64,), jnp.int32),
                pltpu.SemaphoreType.DMA((NY,)),
                pltpu.SemaphoreType.DMA,
            ]
            + [pltpu.VMEM(half, bf16), pltpu.SemaphoreType.DMA((NY,))] * core,
            compiler_params=pltpu.CompilerParams(vmem_limit_bytes=(60 if core else 52) << 20),
            cost_estimate=pl.CostEstimate(flops=1 << 18, bytes_accessed=3 << 19, transcendentals=0),
            name="scale_send" if core else "scale_own",
        )(ranks, grads)

    def local(kernel, out_shape, *operands):
        return pl.pallas_call(
            kernel,
            out_shape=out_shape,
            in_specs=[VMEM] * len(operands),
            out_specs=jax.tree.map(lambda _: VMEM, out_shape),
            compiler_params=PARAMS,
            name=kernel.__name__,
        )(*operands)

    swap = [(0, 1), (1, 0)]
    got = lax.ppermute(scaled(1), "c", swap)
    parts = local(combine_kernel, jax.ShapeDtypeStruct(half, bf16), scaled(0), got)
    parts = lax.all_to_all(parts, "x", 0, 0, tiled=True)
    parts = jnp.sum(parts.astype(f32), axis=0).astype(bf16)
    parts = lax.all_to_all(parts, "y", 0, 0, tiled=True)
    parts = local(spread_kernel, jax.ShapeDtypeStruct((NZ, ROWS, 128), bf16), parts)
    parts = lax.all_to_all(parts, ("zl", "zh"), 0, 0, tiled=True)
    piece = jax.ShapeDtypeStruct((ROWS, 128), bf16)
    weights, grad = local(
        update_kernel, (jax.ShapeDtypeStruct((NS, ROWS, 128), bf16), piece), parts, master, first, second
    )
    mirrors = [
        [(z % NZL) * NS + y * NZH + z // NZL for y in range(NY) for z in (low, NZ - 1 - low)]
        for low in range(NZL)
    ]
    weights = lax.all_to_all(weights, ("zl", "y", "zh"), 0, 0, tiled=True, axis_index_groups=mirrors)
    fan = local(fan_kernel, jax.ShapeDtypeStruct((NX, NS + 1, ROWS, 128), bf16), weights, grad)
    fan = lax.all_to_all(fan, "x", 0, 0, tiled=True)
    other = lax.ppermute(fan, "c", swap)
    out = jax.ShapeDtypeStruct(shard, f32)
    outs = ()
    for partner, ref in enumerate((fan, other)):
        outs = pl.pallas_call(
            functools.partial(finish_kernel, partner),
            out_shape=(jax.ShapeDtypeStruct((NS, NC, NX, ROWS, 128), bf16), out, out, out),
            in_specs=[VMEM] * 4 + [HBM] * len(outs),
            out_specs=(HBM,) * 4,
            input_output_aliases={4 + i: i for i in range(len(outs))},
            scratch_shapes=[
                pltpu.VMEM((3, NX * ROWS, 128), f32),
                pltpu.SemaphoreType.DMA((NX,)),
                pltpu.SemaphoreType.DMA((3,)),
            ],
            compiler_params=PARAMS,
            cost_estimate=pl.CostEstimate(flops=1 << 18, bytes_accessed=3 << 19, transcendentals=0),
            name="finish_partner" if partner else "finish_own",
        )(ref, master, first, second, *outs)
    weights, new_master, new_first, new_second = outs
    return (new_master.reshape(-1), new_first.reshape(-1), new_second.reshape(-1), weights.reshape(-1))


def solution(mesh):
    fine = Mesh(mesh.devices.reshape(NX, NZL, NC, NY, NZH), ("x", "zl", "c", "y", "zh"))
    shard = P(("y", "zh"))
    return jax.shard_map(
        shards,
        mesh=fine,
        in_specs=(P(("x", "zl", "c"), ("y", "zh"), None), shard, shard, shard, P()),
        out_specs=(shard, shard, shard, P()),
        check_vma=False,
    )
```

```python
import functools

import jax
import jax.numpy as jnp
from jax import lax
from jax.experimental import pallas as pl
from jax.experimental.pallas import tpu as pltpu
from jax.sharding import Mesh, PartitionSpec as P

STEP = 1000
bf16, f32 = jnp.bfloat16, jnp.float32
VMEM = pl.BlockSpec(memory_space=pltpu.VMEM)
HBM = pl.BlockSpec(memory_space=pltpu.HBM)
PARAMS = pltpu.CompilerParams(vmem_limit_bytes=8 << 20)

NX, NY, NC, NZL, NZH = 4, 8, 2, 8, 2
NZ = NZL * NZH
NS = NY * NZH
ROWS = 32


def adamw_update(grad, master, first_moment, second_moment):
    new_first = 0.9 * first_moment + 0.1 * grad
    new_second = 0.95 * second_moment + 0.05 * grad * grad
    corr_first = 1.0 - 0.9**STEP
    corr_second = 1.0 - 0.95**STEP
    direction = new_first / corr_first / (jnp.sqrt(new_second / corr_second) + 1e-05)
    new_master = master - 0.05 * (direction + 0.1 * master)
    return (new_master, new_first, new_second)


def scale_kernel(core, ranks, grads, out, buf, rank, sem, rank_sem):
    x, zl, c = lax.axis_index("x"), lax.axis_index("zl"), lax.axis_index("c")
    half = 1 - c if core else c
    copies = [pltpu.make_async_copy(grads.at[y, :, half], buf.at[y], sem.at[y]) for y in range(NY)]
    rank_copy = pltpu.make_async_copy(ranks, rank, rank_sem)
    rank_copy.start()
    for copy in copies:
        copy.start()
    rank_copy.wait()
    outer = (x * NZL + zl) * NC + c
    weight = 1.0 + rank[outer].astype(f32) * (2.0 / 63.0)
    for y in range(NY):
        copies[y].wait()
        for k in range(NX):
            for z in range(NZH):
                out[k, y, z] = (buf[y, z, pl.ds(k * ROWS, ROWS)] * weight).astype(bf16)


def combine_kernel(own, got, out):
    for x in range(NX):
        out[x] = (own[x].astype(f32) + got[x].astype(f32)).astype(bf16)


def spread_kernel(parts, out):
    total = parts[0].astype(f32)
    for y in range(1, NY):
        total += parts[y].astype(f32)
    total = total.astype(bf16)
    for z in range(NZ):
        out[z] = total[z // NZL]


def update_kernel(parts, master, first, second, weights, grad):
    at = pl.ds(pl.multiple_of((lax.axis_index("c") * NX + lax.axis_index("x")) * ROWS, ROWS), ROWS)
    total = parts[0].astype(f32)
    for z in range(1, NZ):
        total += parts[z].astype(f32)
    total = total.astype(bf16)
    grad[...] = total
    piece = adamw_update(total.astype(f32), master[at], first[at], second[at])[0].astype(bf16)
    for s in range(NS):
        weights[s] = piece


def fan_kernel(weights, grad, out):
    for x in range(NX):
        out[x, pl.ds(0, NS)] = weights[...]
        out[x, NS] = grad[...]


def finish_kernel(partner, *refs):
    ref, master, first, second, *_, weights, new_master, new_first, new_second, state, sem, state_sem = refs
    half = lax.axis_index("c")
    half = 1 - half if partner else half
    copies = [
        pltpu.make_async_copy(ref.at[x, pl.ds(0, NS)], weights.at[:, half, x], sem.at[x]) for x in range(NX)
    ]
    for copy in copies:
        copy.start()
    rows = pl.ds(pl.multiple_of(half * NX * ROWS, ROWS), NX * ROWS)
    for x in range(NX):
        at = pl.ds(pl.multiple_of((half * NX + x) * ROWS, ROWS), ROWS)
        new = adamw_update(ref[x, NS].astype(f32), master[at], first[at], second[at])
        for i in range(3):
            state[i, pl.ds(x * ROWS, ROWS)] = new[i]
    for i, out in enumerate((new_master, new_first, new_second)):
        copies.append(pltpu.make_async_copy(state.at[i], out.at[rows], state_sem.at[i]))
        copies[-1].start()
    for copy in copies:
        copy.wait()


def shards(grads, master, first_moment, second_moment, ranks):
    shard = (NC * NX * ROWS, 128)
    master, first, second = (a.reshape(shard) for a in (master, first_moment, second_moment))
    grads = grads.reshape((NY, NZH, NC, NX * ROWS, 128))

    def scaled(core):
        return pl.pallas_call(
            functools.partial(scale_kernel, core),
            out_shape=jax.ShapeDtypeStruct((NX, NY, NZH, ROWS, 128), bf16),
            in_specs=[HBM, HBM],
            out_specs=VMEM,
            scratch_shapes=[
                pltpu.VMEM((NY, NZH, NX * ROWS, 128), f32),
                pltpu.SMEM((64,), jnp.int32),
                pltpu.SemaphoreType.DMA((NY,)),
                pltpu.SemaphoreType.DMA,
            ],
            compiler_params=pltpu.CompilerParams(vmem_limit_bytes=(60 if core else 52) << 20),
            cost_estimate=pl.CostEstimate(flops=1 << 18, bytes_accessed=3 << 19, transcendentals=0),
            name="scale_send" if core else "scale_own",
        )(ranks, grads)

    def local(kernel, out_shape, *operands):
        return pl.pallas_call(
            kernel,
            out_shape=out_shape,
            in_specs=[VMEM] * len(operands),
            out_specs=jax.tree.map(lambda _: VMEM, out_shape),
            compiler_params=PARAMS,
            name=kernel.__name__,
        )(*operands)

    swap = [(0, 1), (1, 0)]
    got = lax.ppermute(scaled(1), "c", swap)
    half = jax.ShapeDtypeStruct((NX, NY, NZH, ROWS, 128), bf16)
    parts = local(combine_kernel, half, scaled(0), got)
    parts = lax.all_to_all(parts, "x", 0, 0, tiled=True)
    parts = jnp.sum(parts.astype(f32), axis=0).astype(bf16)
    parts = lax.all_to_all(parts, "y", 0, 0, tiled=True)
    parts = local(spread_kernel, jax.ShapeDtypeStruct((NZ, ROWS, 128), bf16), parts)
    ring = [[(z % NZL) * NZH + z // NZL for z in range(NZ)]]
    parts = lax.all_to_all(parts, ("zl", "zh"), 0, 0, tiled=True, axis_index_groups=ring)
    piece = jax.ShapeDtypeStruct((ROWS, 128), bf16)
    weights, grad = local(
        update_kernel, (jax.ShapeDtypeStruct((NS, ROWS, 128), bf16), piece), parts, master, first, second
    )
    mirrors = [
        [(z % NZL) * NS + y * NZH + z // NZL for y in range(NY) for z in (low, NZ - 1 - low)]
        for low in range(NZL)
    ]
    weights = lax.all_to_all(weights, ("zl", "y", "zh"), 0, 0, tiled=True, axis_index_groups=mirrors)
    fan = local(fan_kernel, jax.ShapeDtypeStruct((NX, NS + 1, ROWS, 128), bf16), weights, grad)
    fan = lax.all_to_all(fan, "x", 0, 0, tiled=True)
    other = lax.ppermute(fan, "c", swap)
    out = jax.ShapeDtypeStruct(shard, f32)
    outs = ()
    for partner, ref in enumerate((fan, other)):
        outs = pl.pallas_call(
            functools.partial(finish_kernel, partner),
            out_shape=(jax.ShapeDtypeStruct((NS, NC, NX, ROWS, 128), bf16), out, out, out),
            in_specs=[VMEM] * 4 + [HBM] * len(outs),
            out_specs=(HBM,) * 4,
            input_output_aliases={4 + i: i for i in range(len(outs))},
            scratch_shapes=[
                pltpu.VMEM((3, NX * ROWS, 128), f32),
                pltpu.SemaphoreType.DMA((NX,)),
                pltpu.SemaphoreType.DMA((3,)),
            ],
            compiler_params=PARAMS,
            cost_estimate=pl.CostEstimate(flops=1 << 18, bytes_accessed=3 << 19, transcendentals=0),
            name="finish_partner" if partner else "finish_own",
        )(ref, master, first, second, *outs)
    weights, new_master, new_first, new_second = outs
    return (new_master.reshape(-1), new_first.reshape(-1), new_second.reshape(-1), weights.reshape(-1))


def solution(mesh):
    fine = Mesh(mesh.devices.reshape(NX, NZL, NC, NY, NZH), ("x", "zl", "c", "y", "zh"))
    shard = P(("y", "zh"))
    return jax.shard_map(
        shards,
        mesh=fine,
        in_specs=(P(("x", "zl", "c"), ("y", "zh"), None), shard, shard, shard, P()),
        out_specs=(shard, shard, shard, P()),
        check_vma=False,
    )
```

```python
import functools

import jax
import jax.numpy as jnp
from jax import lax
from jax.experimental import pallas as pl
from jax.experimental.pallas import tpu as pltpu
from jax.sharding import Mesh, PartitionSpec as P

STEP = 1000
bf16, f32 = jnp.bfloat16, jnp.float32
VMEM = pl.BlockSpec(memory_space=pltpu.VMEM)
HBM = pl.BlockSpec(memory_space=pltpu.HBM)
PARAMS = pltpu.CompilerParams(vmem_limit_bytes=8 << 20)

NX, NY, NC, NZL, NZH = 4, 8, 2, 8, 2
NZ = NZL * NZH
NS = NY * NZH
ROWS = 32


def adamw_update(grad, master, first_moment, second_moment):
    new_first = 0.9 * first_moment + 0.1 * grad
    new_second = 0.95 * second_moment + 0.05 * grad * grad
    corr_first = 1.0 - 0.9**STEP
    corr_second = 1.0 - 0.95**STEP
    direction = new_first / corr_first / (jnp.sqrt(new_second / corr_second) + 1e-05)
    new_master = master - 0.05 * (direction + 0.1 * master)
    return (new_master, new_first, new_second)


def scale_kernel(core, ranks, grads, out, buf, rank, sem, rank_sem, *send):
    x, zl, c = lax.axis_index("x"), lax.axis_index("zl"), lax.axis_index("c")
    half = 1 - c if core else c
    copies = [pltpu.make_async_copy(grads.at[y, :, half], buf.at[y], sem.at[y]) for y in range(NY)]
    rank_copy = pltpu.make_async_copy(ranks, rank, rank_sem)
    rank_copy.start()
    for copy in copies:
        copy.start()
    rank_copy.wait()
    outer = (x * NZL + zl) * NC + c
    weight = 1.0 + rank[outer].astype(f32) * (2.0 / 63.0)
    stage = send[0] if core else out
    sends = []
    for y in range(NY):
        copies[y].wait()
        for k in range(NX):
            for z in range(NZH):
                stage[k, y, z] = (buf[y, z, pl.ds(k * ROWS, ROWS)] * weight).astype(bf16)
        if core:
            sends.append(pltpu.make_async_copy(stage.at[:, y], out.at[:, y], send[1].at[y]))
            sends[-1].start()
    for copy in sends:
        copy.wait()


def combine_kernel(own, got, out):
    for x in range(NX):
        out[x] = (own[x].astype(f32) + got[x].astype(f32)).astype(bf16)


def spread_kernel(parts, out):
    total = parts[0].astype(f32)
    for y in range(1, NY):
        total += parts[y].astype(f32)
    total = total.astype(bf16)
    for z in range(NZ):
        out[z] = total[z // NZL]


def update_kernel(parts, master, first, second, weights, grad):
    at = pl.ds(pl.multiple_of((lax.axis_index("c") * NX + lax.axis_index("x")) * ROWS, ROWS), ROWS)
    total = parts[0].astype(f32)
    for z in range(1, NZ):
        total += parts[z].astype(f32)
    total = total.astype(bf16)
    grad[...] = total
    piece = adamw_update(total.astype(f32), master[at], first[at], second[at])[0].astype(bf16)
    for s in range(NS):
        weights[s] = piece


def fan_kernel(weights, grad, out):
    for x in range(NX):
        out[x, pl.ds(0, NS)] = weights[...]
        out[x, NS] = grad[...]


def finish_kernel(partner, *refs):
    ref, master, first, second, *_, weights, new_master, new_first, new_second, state, sem, state_sem = refs
    half = lax.axis_index("c")
    half = 1 - half if partner else half
    copies = [
        pltpu.make_async_copy(ref.at[x, pl.ds(0, NS)], weights.at[:, half, x], sem.at[x]) for x in range(NX)
    ]
    for copy in copies:
        copy.start()
    rows = pl.ds(pl.multiple_of(half * NX * ROWS, ROWS), NX * ROWS)
    for x in range(NX):
        at = pl.ds(pl.multiple_of((half * NX + x) * ROWS, ROWS), ROWS)
        new = adamw_update(ref[x, NS].astype(f32), master[at], first[at], second[at])
        for i in range(3):
            state[i, pl.ds(x * ROWS, ROWS)] = new[i]
    for i, out in enumerate((new_master, new_first, new_second)):
        copies.append(pltpu.make_async_copy(state.at[i], out.at[rows], state_sem.at[i]))
        copies[-1].start()
    for copy in copies:
        copy.wait()


def shards(grads, master, first_moment, second_moment, ranks):
    shard = (NC * NX * ROWS, 128)
    master, first, second = (a.reshape(shard) for a in (master, first_moment, second_moment))
    grads = grads.reshape((NY, NZH, NC, NX * ROWS, 128))

    half = (NX, NY, NZH, ROWS, 128)

    def scaled(core):
        return pl.pallas_call(
            functools.partial(scale_kernel, core),
            out_shape=jax.ShapeDtypeStruct(half, bf16),
            in_specs=[HBM, HBM],
            out_specs=HBM if core else VMEM,
            scratch_shapes=[
                pltpu.VMEM((NY, NZH, NX * ROWS, 128), f32),
                pltpu.SMEM((64,), jnp.int32),
                pltpu.SemaphoreType.DMA((NY,)),
                pltpu.SemaphoreType.DMA,
            ]
            + [pltpu.VMEM(half, bf16), pltpu.SemaphoreType.DMA((NY,))] * core,
            compiler_params=pltpu.CompilerParams(vmem_limit_bytes=(60 if core else 52) << 20),
            cost_estimate=pl.CostEstimate(flops=1 << 18, bytes_accessed=3 << 19, transcendentals=0),
            name="scale_send" if core else "scale_own",
        )(ranks, grads)

    def local(kernel, out_shape, *operands):
        return pl.pallas_call(
            kernel,
            out_shape=out_shape,
            in_specs=[VMEM] * len(operands),
            out_specs=jax.tree.map(lambda _: VMEM, out_shape),
            compiler_params=PARAMS,
            name=kernel.__name__,
        )(*operands)

    swap = [(0, 1), (1, 0)]
    got = lax.ppermute(scaled(1), "c", swap)
    parts = local(combine_kernel, jax.ShapeDtypeStruct(half, bf16), scaled(0), got)
    parts = lax.all_to_all(parts, "x", 0, 0, tiled=True)
    parts = jnp.sum(parts.astype(f32), axis=0).astype(bf16)
    parts = lax.all_to_all(parts, "y", 0, 0, tiled=True)
    parts = local(spread_kernel, jax.ShapeDtypeStruct((NZ, ROWS, 128), bf16), parts)
    ring = [[(z % NZL) * NZH + z // NZL for z in range(NZ)]]
    parts = lax.all_to_all(parts, ("zl", "zh"), 0, 0, tiled=True, axis_index_groups=ring)
    piece = jax.ShapeDtypeStruct((ROWS, 128), bf16)
    weights, grad = local(
        update_kernel, (jax.ShapeDtypeStruct((NS, ROWS, 128), bf16), piece), parts, master, first, second
    )
    mirrors = [
        [(z % NZL) * NS + y * NZH + z // NZL for y in range(NY) for z in (low, NZ - 1 - low)]
        for low in range(NZL)
    ]
    weights = lax.all_to_all(weights, ("zl", "y", "zh"), 0, 0, tiled=True, axis_index_groups=mirrors)
    fan = local(fan_kernel, jax.ShapeDtypeStruct((NX, NS + 1, ROWS, 128), bf16), weights, grad)
    fan = lax.all_to_all(fan, "x", 0, 0, tiled=True)
    other = lax.ppermute(fan, "c", swap)
    out = jax.ShapeDtypeStruct(shard, f32)
    outs = ()
    for partner, ref in enumerate((fan, other)):
        outs = pl.pallas_call(
            functools.partial(finish_kernel, partner),
            out_shape=(jax.ShapeDtypeStruct((NS, NC, NX, ROWS, 128), bf16), out, out, out),
            in_specs=[VMEM] * 4 + [HBM] * len(outs),
            out_specs=(HBM,) * 4,
            input_output_aliases={4 + i: i for i in range(len(outs))},
            scratch_shapes=[
                pltpu.VMEM((3, NX * ROWS, 128), f32),
                pltpu.SemaphoreType.DMA((NX,)),
                pltpu.SemaphoreType.DMA((3,)),
            ],
            compiler_params=PARAMS,
            cost_estimate=pl.CostEstimate(flops=1 << 18, bytes_accessed=3 << 19, transcendentals=0),
            name="finish_partner" if partner else "finish_own",
        )(ref, master, first, second, *outs)
    weights, new_master, new_first, new_second = outs
    return (new_master.reshape(-1), new_first.reshape(-1), new_second.reshape(-1), weights.reshape(-1))


def solution(mesh):
    fine = Mesh(mesh.devices.reshape(NX, NZL, NC, NY, NZH), ("x", "zl", "c", "y", "zh"))
    shard = P(("y", "zh"))
    return jax.shard_map(
        shards,
        mesh=fine,
        in_specs=(P(("x", "zl", "c"), ("y", "zh"), None), shard, shard, shard, P()),
        out_specs=(shard, shard, shard, P()),
        check_vma=False,
    )
```
